32 devices in a mesh: clus: 8 (over z, x), blk: 4 (over y, core).
Axes of the slice: x: 2, y: 2, z: 4, core: 2. Of those that a mesh axis runs over, the one named last changes fastest.
Arguments:
- adjoint: bfloat16 [32, 384, 3, 128], P('clus', 'blk'), may hold values from -6 to 6
- blocks: bfloat16 [192, 384, 3, 1152], P('clus', 'blk'), may hold values from -0.1875 to 0.1875
- row_cluster: int32 [192], P('clus'), may hold values from 0 to 3
- col_owner: int32 [192, 1], P('clus'), may hold values from 0 to 7; in each aligned block of 24 rows (0 to 23, 24 to 47, ...) at most 6 rows name the same one
- col_cluster: int32 [192], P('clus'), may hold values from 0 to 3
- tangent: float32 [32, 3, 3, 384], P('clus', None, None, 'blk'), may hold values from -5 to 5
Outputs:
- sensitivity: float32 [32, 384, 3, 128], P('clus', 'blk')
The draws below stay inside these ranges and needn't reach their ends.
Inputs may be any that keep to these rules, and one draw needn't show every extreme that they name: `col_owner`: among the 24 pairs stored by one index of clus (aligned blocks of the list), at most 6 name one owner, a bound that some block reaches of them.
All inputs are finite; a program needn't handle non-finite values.
Results may differ from the reference program's by a relative error of at most 0.0003.
Values sent between devices are 32-bit elements; how exact they have to be, the bound alone decides.
No kernel may reach another device: no remote copies, remote signals or barrier semaphores. Data moves between devices by JAX's collectives and lax.ppermute only.
A program may use at most 192 MiB of HBM per device.

```python
import math
import jax
import jax.numpy as jnp
import numpy as np
from jax import lax

TILES = 384
R = 128
CLUS_DEV = 4
CLUSTER_PAIRS = 24
CAP = 6
NOWNERS = 8
NCLUS = 32
PAIRS = 192


def plant(drawn, key, least, largest):
    shape = drawn.shape
    place = [jax.random.randint(jax.random.fold_in(key, axis), (), 0, shape[axis]) for axis in range(len(shape))]
    drawn = drawn.at[tuple(place)].set(least)
    longest = shape.index(max(shape))
    place[longest] = (place[longest] + 1) % shape[longest]
    return drawn.at[tuple(place)].set(largest)


def shard_levels(stream_key, extent, cuts, low, top_value):
    def one(position, blocks):
        draws = jax.random.uniform(jax.random.fold_in(jax.random.fold_in(stream_key, 6), position), (blocks,), jnp.float32, low / len(cuts), top_value / len(cuts))
        return jnp.repeat(jnp.exp(draws), extent[position] // blocks).reshape((-1,) + (1,) * (len(extent) - position - 1))

    factor_of = one(*cuts[0])
    for cut in cuts[1:]:
        factor_of = factor_of * one(*cut)
    return factor_of


def deal_out(own_key, own, number, rows, amount, top, bound, lean):
    order = jax.random.permutation(own_key, amount)
    packed, usual = load_shares(amount, rows * top, bound, lean, True), load_shares(amount, rows * top, bound, lean, False)
    places = jnp.arange(amount)

    def named(tallies, offset_by):
        used = int((tallies > 0).sum())
        fixed = max(1, used // 4)
        passed = fixed + (places - fixed + offset_by * (used - fixed)) % max(1, amount - fixed)
        return jnp.zeros((amount,), jnp.int32).at[order[jnp.where(places < fixed, places, passed)]].set(jnp.asarray(tallies, jnp.int32))

    tallies = jnp.where(number % 4 == 0, named(packed, number // 4), named(usual, number - number // 4 - 1))
    mixed = jax.random.permutation(jax.random.fold_in(own, 3), amount)
    donor, sink = mixed[0:amount // 2 * 2:2], mixed[1:amount // 2 * 2:2]
    margin = jnp.minimum(tallies[donor] - 1, bound - tallies[sink]) // 2
    margin = jnp.where((donor == order[0]) | (sink == order[0]) | (tallies[sink] == 0), 0, jnp.maximum(margin, 0))
    passed = jax.random.randint(jax.random.fold_in(own, 4), (amount // 2,), 0, 1 << 20) % (margin + 1)
    tallies = tallies.at[donor].add(-passed).at[sink].add(passed)
    labels = jnp.searchsorted(jnp.cumsum(tallies), jnp.arange(rows * top), side="right").astype(jnp.int32)
    listing = labels.reshape(top, rows).T
    listing = listing[jax.random.permutation(jax.random.fold_in(own, 1), rows)]
    offset_by = jax.random.randint(jax.random.fold_in(own, 2), (rows, 1), 0, top)
    return jnp.take_along_axis(listing, (jnp.arange(top)[None, :] + offset_by) % top, axis=1)


def load_shares(amount, total, most, slope, full):
    loads = [(1 << 20) // math.isqrt(standing ** slope) + 1 for standing in range(1, amount + 1)]
    largest = most if full else min(most, max(-(-total // amount), total * loads[0] // sum(loads)))
    least = 1 if total - largest >= amount - 1 else 0
    given, surplus = [largest] + [least] * (amount - 1), total - largest - least * (amount - 1)
    while surplus > 0:
        movable = [i for i in range(1, amount) if given[i] < largest] or [i for i in range(1, amount) if given[i] < most]
        whole, remaining = sum([loads[i] for i in movable]), surplus
        for i in movable:
            addition = min(most - given[i], max(1, remaining * loads[i] // whole), surplus)
            given[i] = given[i] + addition
            surplus = surplus - addition
    return np.array(given)


def scatter_about(rng, extent, width, reach, split=(), held_as=jnp.bfloat16):
    result = jax.random.normal(rng, extent, jnp.float32) * width
    if len(split) > 0:
        result = shard_levels(rng, extent, split, -0.22, 0.18) * result
    return jnp.clip(result, min=-reach, max=reach).astype(held_as)


def setup_inputs(seed: int = 0) -> dict:
    seeds = jax.random.split(jax.random.key(seed), 7)
    adjoint = scatter_about(seeds[0], (NCLUS, TILES, 3, R), 1.0, 6.0, ((0, 8), (1, 4)))
    blocks = scatter_about(seeds[1], (PAIRS, TILES, 3, 3 * TILES), (3 * TILES) ** -0.5, 0.1875, ((0, 8), (1, 4)))
    row_cluster = plant(jax.random.randint(seeds[2], (PAIRS,), 0, CLUS_DEV), jax.random.fold_in(seeds[2], 1), 0, CLUS_DEV - 1).astype(jnp.int32)
    col_owner_keys = jax.random.split(jax.random.fold_in(seeds[3], 1), PAIRS // CLUSTER_PAIRS)
    col_owner_turns = jax.random.permutation(jax.random.fold_in(seeds[3], 3), PAIRS // CLUSTER_PAIRS)
    col_owner = jax.vmap(lambda own, number: deal_out(jax.random.fold_in(seeds[3], 2), own, number, CLUSTER_PAIRS, NOWNERS, 1, CAP, 2))(col_owner_keys, col_owner_turns).reshape((PAIRS, 1))
    col_cluster = plant(jax.random.randint(seeds[4], (PAIRS,), 0, CLUS_DEV), jax.random.fold_in(seeds[4], 1), 0, CLUS_DEV - 1).astype(jnp.int32)
    tangent = scatter_about(seeds[5], (NCLUS, 3, 3, TILES), 1.0, 5.0, ((0, 8), (3, 4)), jnp.float32)
    return {"adjoint": adjoint, "blocks": blocks, "row_cluster": row_cluster, "col_owner": col_owner, "col_cluster": col_cluster, "tangent": tangent}


def reference(adjoint, blocks, row_cluster, col_owner, col_cluster, tangent):
    owner_index = jnp.arange(PAIRS, dtype=jnp.int32) // CLUSTER_PAIRS
    row_index = (owner_index * CLUS_DEV + row_cluster).astype(jnp.int32)
    col_index = (col_owner[:, 0] * CLUS_DEV + col_cluster).astype(jnp.int32)
    flat_adjoint = adjoint.reshape(NCLUS, 3 * TILES, R)

    def add_pair(running_total, scanned):
        block_piece, source, target = scanned
        lam_rows = lax.dynamic_index_in_dim(flat_adjoint, source, 0, keepdims=False).astype(jnp.float32)
        matrix = block_piece.reshape(3 * TILES, 3 * TILES).astype(jnp.float32)
        partial_value = jnp.dot(matrix.T, lam_rows, precision=lax.Precision.HIGHEST)
        present_total = lax.dynamic_index_in_dim(running_total, target, 0, keepdims=False)
        return lax.dynamic_update_index_in_dim(running_total, present_total + partial_value, target, 0), None

    start_field = jnp.zeros((NCLUS, 3 * TILES, R), jnp.float32)
    running_total, unused = lax.scan(add_pair, start_field, (blocks, row_index, col_index))
    field = running_total.reshape(NCLUS, TILES, 3, R)
    results = []
    for out_comp in range(3):
        accum = tangent[:, 0, out_comp, :, None] * field[:, :, 0, :]
        for in_comp in range(1, 3):
            accum = accum + tangent[:, in_comp, out_comp, :, None] * field[:, :, in_comp, :]
        results.append(accum)
    return jnp.stack(results, axis=2)
```

```python
import functools

import jax
import jax.numpy as jnp
from jax import lax
from jax.experimental import pallas as pl
from jax.experimental.pallas import tpu as pltpu
from jax.sharding import PartitionSpec as P


PLAN = ((10, "b120"), (9, "0b12"), (9, "10b2"), (8, "b012"))


def bits_of(size):
    return size.bit_length() - 1


def cut_rows(rows):
    whole = sum(share for share, _ in PLAN)
    edges, total = [0], 0
    for share, _ in PLAN:
        total += share
        edges.append(rows // 8 * total // whole * 8)
    edges[-1] = rows
    return list(zip(edges[:-1], edges[1:]))


def route(order, blk_bits, clus_bits):
    steps = []
    for letter in order:
        if letter == "b":
            steps += [("blk", bit) for bit in range(1, blk_bits)]
        elif int(letter) < clus_bits:
            steps.append(("clus", int(letter)))
    named = [bit for axis, bit in steps if axis == "clus"]
    return steps + [("clus", bit) for bit in range(clus_bits) if bit not in named]


def couple_kernel(cuts, piece, halves, row_ref, side_ref, adjoint_ref, block_ref, *rest):
    outs, result_ref = rest[:-1], rest[-1]
    pair = pl.program_id(0)
    side = side_ref[0]
    lam = adjoint_ref[row_ref[pair]]
    result_ref[...] = lax.dot_general(
        block_ref[0], lam, (((0,), (0,)), ((), ())), preferred_element_type=jnp.float32
    )
    for index, (begin, end) in enumerate(cuts):
        for half in range(halves):
            away = pl.multiple_of((2 * half + 1 - side) * piece + begin, 8)
            home = pl.multiple_of((2 * half + side) * piece + begin, 8)
            outs[2 * index][half, 0] = result_ref[pl.ds(away, end - begin), :]
            outs[2 * index + 1][half, 0] = result_ref[pl.ds(home, end - begin), :]


def couple(adjoint, blocks, row_cluster, side, cuts, piece, halves):
    pairs, depth, width = blocks.shape
    clus_dev, _, right = adjoint.shape
    shapes, specs = [], []
    for begin, end in cuts:
        for _ in range(2):
            shapes.append(jax.ShapeDtypeStruct((halves, pairs, end - begin, right), jnp.float32))
            specs.append(
                pl.BlockSpec((halves, 1, end - begin, right), lambda p, rows, side: (0, p, 0, 0))
            )
    flat = pl.pallas_call(
        functools.partial(couple_kernel, cuts, piece, halves),
        out_shape=shapes,
        grid_spec=pltpu.PrefetchScalarGridSpec(
            num_scalar_prefetch=2,
            grid=(pairs,),
            in_specs=[
                pl.BlockSpec((clus_dev, depth, right), lambda p, rows, side: (0, 0, 0)),
                pl.BlockSpec((1, depth, width), lambda p, rows, side: (p, 0, 0)),
            ],
            out_specs=specs,
            scratch_shapes=[pltpu.VMEM((width, right), jnp.float32)],
        ),
        name="couple",
        cost_estimate=pl.CostEstimate(
            flops=2 * pairs * depth * width * right,
            bytes_accessed=pairs * width * (2 * depth + 4 * right),
            transcendentals=0,
        ),
    )(row_cluster, side, adjoint, blocks)
    return [(flat[2 * k], flat[2 * k + 1]) for k in range(len(cuts))]


def gather_kernel(slot_ref, keep_ref, recv_ref, send_ref, home_ref, total_ref):
    total_ref[...] = jnp.zeros_like(total_ref)

    def add(pair, carry):
        slot = slot_ref[pair]
        total_ref[slot] += keep_ref[0, pair] + recv_ref[0, pair]
        return carry

    lax.fori_loop(0, keep_ref.shape[1], add, 0)
    half = send_ref.shape[1]
    send_ref[0] = total_ref[:half]
    home_ref[0] = total_ref[half:]


def row_step(rows):
    best = 8
    for step in range(8, min(rows, 48) + 1, 8):
        if rows % step == 0:
            best = step
    return best


def gather_slots(slots, keep, recv, half):
    lead, pairs, rows, right = keep.shape
    step = row_step(rows)
    shape = jax.ShapeDtypeStruct((lead, half, rows, right), jnp.float32)
    read = pl.BlockSpec((1, pairs, step, right), lambda a, r, s: (a, 0, r, 0))
    write = pl.BlockSpec((1, half, step, right), lambda a, r, s: (a, 0, r, 0))
    return pl.pallas_call(
        gather_kernel,
        out_shape=[shape, shape],
        grid_spec=pltpu.PrefetchScalarGridSpec(
            num_scalar_prefetch=1,
            grid=(lead, rows // step),
            in_specs=[read, read],
            out_specs=[write, write],
            scratch_shapes=[pltpu.VMEM((2 * half, step, right), jnp.float32)],
        ),
        name="gather_slots",
        cost_estimate=pl.CostEstimate(
            flops=2 * keep.size, bytes_accessed=8 * keep.size + 8 * lead * half * rows * right,
            transcendentals=0,
        ),
    )(slots, keep, recv)


def finish_kernel(cuts, tangent_ref, *rest):
    parts, out_ref, field_ref = rest[:-2], rest[-2], rest[-1]
    for index, (begin, end) in enumerate(cuts):
        field_ref[begin:end] = parts[2 * index][0] + parts[2 * index + 1][0]
    tiles = out_ref.shape[2]
    field = [field_ref[pl.ds(comp, tiles, stride=3), :] for comp in range(3)]
    for out_comp in range(3):
        accum = tangent_ref[0, :, out_comp : out_comp + 1] * field[0]
        for in_comp in range(1, 3):
            place = 3 * in_comp + out_comp
            accum = accum + tangent_ref[0, :, place : place + 1] * field[in_comp]
        out_ref[0, out_comp] = accum


def finish(tangent, parts, cuts, piece):
    clus_dev, tiles, nine = tangent.shape
    right = parts[0].shape[-1]
    specs = [pl.BlockSpec((1, tiles, nine), lambda c: (c, 0, 0))]
    for part in parts:
        specs.append(pl.BlockSpec((1, part.shape[1], right), lambda c: (c, 0, 0)))
    return pl.pallas_call(
        functools.partial(finish_kernel, cuts),
        out_shape=jax.ShapeDtypeStruct((clus_dev, 3, tiles, right), jnp.float32),
        grid=(clus_dev,),
        in_specs=specs,
        out_specs=pl.BlockSpec((1, 3, tiles, right), lambda c: (c, 0, 0, 0)),
        scratch_shapes=[pltpu.VMEM((piece, right), jnp.float32)],
        name="finish",
        cost_estimate=pl.CostEstimate(
            flops=18 * clus_dev * tiles * right,
            bytes_accessed=48 * clus_dev * tiles * right,
            transcendentals=0,
        ),
    )(tangent, *parts)


def local(adjoint, blocks, row_cluster, col_owner, col_cluster, tangent):
    pairs, tiles, comps, width = blocks.shape
    clus_dev, right = adjoint.shape[0], adjoint.shape[3]
    sizes = {"clus": lax.axis_size("clus"), "blk": lax.axis_size("blk")}
    here = {"clus": lax.axis_index("clus"), "blk": lax.axis_index("blk")}
    clus_bits, blk_bits = bits_of(sizes["clus"]), bits_of(sizes["blk"])
    piece = width // sizes["blk"]
    halves = sizes["blk"] // 2
    cuts = cut_rows(piece)
    owner = col_owner[:, 0]

    def my_bit(axis, bit):
        return (here[axis] >> bit) & 1

    def swap(value, axis, bit):
        return lax.ppermute(value, axis, [(i, i ^ (1 << bit)) for i in range(sizes[axis])])

    flat_adjoint = adjoint.transpose(0, 2, 1, 3).reshape(clus_dev, comps * tiles, right)
    flat_blocks = blocks.transpose(0, 2, 1, 3).reshape(pairs, comps * tiles, width)
    side = my_bit("blk", 0).astype(jnp.int32).reshape(1)
    chunks = couple(flat_adjoint, flat_blocks, row_cluster, side, cuts, piece, halves)
    half = sizes["clus"] * clus_dev // 2

    def slots_for(bit):
        apart = (owner >> bit) & 1
        other = ((owner >> (bit + 1)) << bit) | (owner & ((1 << bit) - 1))
        home = (apart == my_bit("clus", bit)).astype(jnp.int32)
        return home * half + other * clus_dev + col_cluster

    parts = []
    state = []
    for (send, keep), (_, order) in zip(chunks, PLAN):
        labels = [("blk", bit) for bit in range(blk_bits - 1, 0, -1)] + ["pairs"]
        state.append([keep, swap(send, "blk", 0), labels, route(order, blk_bits, clus_bits)])
    for step in range(len(state[0][3])):
        for entry in state:
            keep, recv, labels, steps = entry
            rows = keep.shape[-2]
            axis, bit = steps[step]
            if axis == "clus" and "pairs" in labels:
                lead = 2 ** (len(labels) - 1)
                send, home = gather_slots(
                    slots_for(bit),
                    keep.reshape(lead, pairs, rows, right),
                    recv.reshape(lead, pairs, rows, right),
                    half,
                )
                labels = labels[:-1] + [
                    ("clus", b) for b in range(clus_bits - 1, -1, -1) if b != bit
                ] + ["own"]
            else:
                place = labels.index((axis, bit))
                lead = 2**place
                both = (keep.reshape(lead, 2, -1, rows, right), recv.reshape(lead, 2, -1, rows, right))
                mine = my_bit(axis, bit)

                def pick(which):
                    left, other = (
                        lax.dynamic_index_in_dim(v, which, 1, keepdims=False) for v in both
                    )
                    return left + other

                send, home = pick(1 - mine), pick(mine)
                labels = labels[:place] + labels[place + 1 :]
            entry[0] = home
            entry[1] = swap(send, axis, bit).reshape(home.shape)
            entry[2] = labels
    for keep, recv, _, _ in state:
        parts += [keep.reshape(clus_dev, -1, right), recv.reshape(clus_dev, -1, right)]
    turned = tangent.transpose(0, 3, 1, 2).reshape(clus_dev, tiles, 9)
    out = finish(turned, parts, cuts, piece)
    return out.transpose(0, 2, 1, 3)


def solution(mesh):
    placed = (
        P("clus", "blk", None, None),
        P("clus", "blk", None, None),
        P("clus"),
        P("clus", None),
        P("clus"),
        P("clus", None, None, "blk"),
    )
    return jax.shard_map(
        local, mesh=mesh, in_specs=placed, out_specs=P("clus", "blk", None, None), check_vma=False
    )
```

```python
import functools

import jax
import jax.numpy as jnp
from jax import lax
from jax.experimental import pallas as pl
from jax.experimental.pallas import tpu as pltpu
from jax.sharding import PartitionSpec as P


PLAN = ((9, '10b2'), (8, 'b102'), (10, 'b120'), (9, '0b12'))

EVENTS = ('couple', (2, 0), (0, None), (3, None), (1, 0), (2, None), (0, None), (3, None), (1, None), (2, None), (0, None), (3, None), (1, None), (0, None), (2, None), (1, None), (3, None))

PER = 2
PARTS = 1
VMEM_BYTES = 67043328


def bits_of(size):
    return size.bit_length() - 1


def cut_rows(rows):
    whole = sum(share for share, _ in PLAN)
    edges, total = [0], 0
    for share, _ in PLAN:
        total += share
        edges.append(rows // 8 * total // whole * 8)
    edges[-1] = rows
    return list(zip(edges[:-1], edges[1:]))


def route(order, blk_bits, clus_bits):
    steps = []
    for letter in order:
        if letter == "b":
            steps += [("blk", bit) for bit in range(1, blk_bits)]
        elif int(letter) < clus_bits:
            steps.append(("clus", int(letter)))
    named = [bit for axis, bit in steps if axis == "clus"]
    return steps + [("clus", bit) for bit in range(clus_bits) if bit not in named]


def couple_kernel(cuts, piece, halves, aliased, row_ref, side_ref, adjoint_ref, block_ref, *rest):
    outs, result_ref = rest[aliased:-1], rest[-1]
    per = block_ref.shape[0]
    first = pl.program_id(0) * per
    side = side_ref[0]
    for inner in range(per):
        lam = adjoint_ref[row_ref[first + inner]]
        result_ref[inner] = lax.dot_general(
            block_ref[inner], lam, (((0,), (0,)), ((), ())), preferred_element_type=jnp.float32
        )
        for index, (begin, end) in enumerate(cuts):
            for half in range(halves):
                away = pl.multiple_of((2 * half + 1 - side) * piece + begin, 8)
                home = pl.multiple_of((2 * half + side) * piece + begin, 8)
                outs[2 * index][half, inner] = result_ref[inner, pl.ds(away, end - begin), :]
                outs[2 * index + 1][half, inner] = result_ref[inner, pl.ds(home, end - begin), :]


def couple(adjoint, blocks, rows, side, cuts, early, piece, halves, part, held):
    pairs, depth, width = blocks.shape
    clus_dev, _, right = adjoint.shape
    count = rows.shape[0]
    per = next(n for n in (PER, 2, 1) if count % n == 0)
    jump = part * count // per
    shapes, specs, aliases, extra = [], [], {}, []
    for (begin, end), alone in zip(cuts, early):
        for _ in range(2):
            shape = (halves, count if alone else pairs, end - begin, right)
            if not alone and part > 0:
                aliases[4 + len(extra)] = len(shapes)
                extra.append(held[len(shapes)])
            shapes.append(jax.ShapeDtypeStruct(shape, jnp.float32))
            move = 0 if alone else jump
            specs.append(
                pl.BlockSpec(
                    (halves, per, end - begin, right),
                    lambda p, rows, side, move=move: (0, p + move, 0, 0),
                )
            )
    grant = VMEM_BYTES - blocks.size * blocks.dtype.itemsize * 15 // 16
    return pl.pallas_call(
        functools.partial(couple_kernel, cuts, piece, halves, len(extra)),
        out_shape=shapes,
        grid_spec=pltpu.PrefetchScalarGridSpec(
            num_scalar_prefetch=2,
            grid=(count // per,),
            in_specs=[
                pl.BlockSpec((clus_dev, depth, right), lambda p, rows, side: (0, 0, 0)),
                pl.BlockSpec((per, depth, width), lambda p, rows, side: (p + jump, 0, 0)),
            ]
            + [pl.BlockSpec(memory_space=pl.ANY)] * len(extra),
            out_specs=specs,
            scratch_shapes=[pltpu.VMEM((per, width, right), jnp.float32)],
        ),
        input_output_aliases=aliases,
        name="couple",
        compiler_params=pltpu.CompilerParams(vmem_limit_bytes=grant),
        cost_estimate=pl.CostEstimate(
            flops=2 * count * depth * width * right,
            bytes_accessed=count * width * (2 * depth + 4 * right),
            transcendentals=0,
        ),
    )(rows, side, adjoint, blocks, *extra)


def gather_kernel(parts, slot_ref, *rest):
    values, (send_ref, home_ref, total_ref) = rest[: 2 * parts], rest[2 * parts :]
    total_ref[...] = jnp.zeros_like(total_ref)
    for part in range(parts):
        keep_ref, recv_ref = values[2 * part], values[2 * part + 1]
        count = keep_ref.shape[1]

        def add(pair, carry):
            slot = slot_ref[part * count + pair]
            total_ref[slot] += keep_ref[0, pair] + recv_ref[0, pair]
            return carry

        lax.fori_loop(0, count, add, 0, unroll=4)
    half = send_ref.shape[1]
    send_ref[0] = total_ref[:half]
    home_ref[0] = total_ref[half:]


def row_step(rows):
    best = 8
    for step in range(8, min(rows, 96) + 1, 8):
        if rows % step == 0:
            best = step
    return best


def gather_slots(slots, values, half):
    lead, count, rows, right = values[0].shape
    pairs = slots.shape[0]
    step = row_step(rows)
    shape = jax.ShapeDtypeStruct((lead, half, rows, right), jnp.float32)
    read = pl.BlockSpec((1, count, step, right), lambda a, r, s: (a, 0, r, 0))
    write = pl.BlockSpec((1, half, step, right), lambda a, r, s: (a, 0, r, 0))
    grant = 16 * step * right * (2 * pairs + 3 * half) + (2 << 20)
    return pl.pallas_call(
        functools.partial(gather_kernel, len(values) // 2),
        out_shape=[shape, shape],
        grid_spec=pltpu.PrefetchScalarGridSpec(
            num_scalar_prefetch=1,
            grid=(lead, rows // step),
            in_specs=[read] * len(values),
            out_specs=[write, write],
            scratch_shapes=[pltpu.VMEM((2 * half, step, right), jnp.float32)],
        ),
        name="gather_slots",
        compiler_params=pltpu.CompilerParams(vmem_limit_bytes=grant),
        cost_estimate=pl.CostEstimate(
            flops=2 * lead * pairs * rows * right,
            bytes_accessed=8 * lead * (pairs + half) * rows * right,
            transcendentals=0,
        ),
    )(slots, *values)


def finish_kernel(cuts, tangent_ref, *rest):
    parts, out_ref, field_ref = rest[:-2], rest[-2], rest[-1]
    for index, (begin, end) in enumerate(cuts):
        field_ref[begin:end] = parts[2 * index][0] + parts[2 * index + 1][0]
    tiles = out_ref.shape[2]
    field = [field_ref[pl.ds(comp, tiles, stride=3), :] for comp in range(3)]
    for out_comp in range(3):
        accum = tangent_ref[0, :, out_comp : out_comp + 1] * field[0]
        for in_comp in range(1, 3):
            place = 3 * in_comp + out_comp
            accum = accum + tangent_ref[0, :, place : place + 1] * field[in_comp]
        out_ref[0, out_comp] = accum


def finish(tangent, parts, cuts, piece):
    clus_dev, tiles, nine = tangent.shape
    right = parts[0].shape[-1]
    specs = [pl.BlockSpec((1, tiles, nine), lambda c: (c, 0, 0))]
    for part in parts:
        specs.append(pl.BlockSpec((1, part.shape[1], right), lambda c: (c, 0, 0)))
    return pl.pallas_call(
        functools.partial(finish_kernel, cuts),
        out_shape=jax.ShapeDtypeStruct((clus_dev, 3, tiles, right), jnp.float32),
        grid=(clus_dev,),
        in_specs=specs,
        out_specs=pl.BlockSpec((1, 3, tiles, right), lambda c: (c, 0, 0, 0)),
        scratch_shapes=[pltpu.VMEM((piece, right), jnp.float32)],
        name="finish",
        compiler_params=pltpu.CompilerParams(vmem_limit_bytes=8 << 20),
        cost_estimate=pl.CostEstimate(
            flops=18 * clus_dev * tiles * right,
            bytes_accessed=48 * clus_dev * tiles * right,
            transcendentals=0,
        ),
    )(tangent, *parts)


def local(adjoint, blocks, row_cluster, col_owner, col_cluster, tangent):
    pairs, tiles, comps, width = blocks.shape
    clus_dev, right = adjoint.shape[0], adjoint.shape[3]
    sizes = {"clus": lax.axis_size("clus"), "blk": lax.axis_size("blk")}
    here = {"clus": lax.axis_index("clus"), "blk": lax.axis_index("blk")}
    clus_bits, blk_bits = bits_of(sizes["clus"]), bits_of(sizes["blk"])
    piece = width // sizes["blk"]
    halves = sizes["blk"] // 2
    cuts = cut_rows(piece)
    owner = col_owner[:, 0]

    def my_bit(axis, bit):
        return (here[axis] >> bit) & 1

    def swap(value, axis, bit):
        return lax.ppermute(value, axis, [(i, i ^ (1 << bit)) for i in range(sizes[axis])])

    flat_adjoint = adjoint.transpose(0, 2, 1, 3).reshape(clus_dev, comps * tiles, right)
    flat_blocks = blocks.transpose(0, 2, 1, 3).reshape(pairs, comps * tiles, width)
    side = my_bit("blk", 0).astype(jnp.int32).reshape(1)
    half = sizes["clus"] * clus_dev // 2
    routes = [route(order, blk_bits, clus_bits) for _, order in PLAN]
    early = [steps[0][0] == "blk" for steps in routes]
    parts = next(n for n in (PARTS, 2, 1) if pairs % n == 0)
    count = pairs // parts

    def slots_for(bit):
        apart = (owner >> bit) & 1
        other = ((owner >> (bit + 1)) << bit) | (owner & ((1 << bit) - 1))
        home = (apart == my_bit("clus", bit)).astype(jnp.int32)
        return home * half + other * clus_dev + col_cluster

    def split(keep, recv, lead, axis, bit):
        rows = keep.shape[-2]
        both = [v.reshape(lead, 2, -1, rows, right) for v in (keep, recv)]
        mine = my_bit(axis, bit)

        def pick(which):
            left, other = (lax.dynamic_index_in_dim(v, which, 1, keepdims=False) for v in both)
            return left + other

        send, home = pick(1 - mine), pick(mine)
        recv = swap(send, axis, bit)
        return home, recv.reshape(home.shape)

    state = [None] * len(PLAN)
    used = [event[0] for event in EVENTS if event != "couple"]
    first_use = sorted(range(len(PLAN)), key=lambda c: used.index(c) if c in used else len(used))
    held = None

    def run_couple(part):
        nonlocal held
        rows = lax.slice_in_dim(row_cluster, part * count, (part + 1) * count)
        held = couple(flat_adjoint, flat_blocks, rows, side, cuts, early, piece, halves, part, held)
        for chunk in first_use:
            send, keep = held[2 * chunk], held[2 * chunk + 1]
            if early[chunk] or part == parts - 1:
                recv = swap(send, "blk", 0)
                state[chunk] = (state[chunk] or []) + [(keep, recv)]

    labels = [[("blk", bit) for bit in range(blk_bits - 1, 0, -1)] + ["pairs"] for _ in PLAN]
    done = {}

    def run(chunk, part=None):
        place = done.get((chunk, part), done.get((chunk, None), 0))
        if part is not None and (
            (chunk, part) in done or "pairs" not in labels[chunk] or part >= len(state[chunk])
        ):
            return
        if place >= len(routes[chunk]):
            return
        axis, bit = routes[chunk][place]
        if axis == "clus" and "pairs" in labels[chunk]:
            values = []
            for pair in state[chunk]:
                values += [v.reshape(-1, *v.shape[-3:]) for v in pair]
            slots = slots_for(bit)
            send, home = gather_slots(slots, values, half)
            recv = swap(send, axis, bit)
            labels[chunk] = labels[chunk][:-1] + [
                ("clus", b) for b in range(clus_bits - 1, -1, -1) if b != bit
            ] + ["own"]
            state[chunk] = [(home, recv)]
        else:
            spot = labels[chunk].index((axis, bit))
            which = range(len(state[chunk])) if part is None else [part]
            for index in which:
                if (chunk, index) in done and part is None and "pairs" in labels[chunk]:
                    continue
                state[chunk][index] = split(*state[chunk][index], 2**spot, axis, bit)
                if "pairs" in labels[chunk]:
                    done[(chunk, index)] = place + 1
            if "pairs" in labels[chunk] and len(
                [i for i in range(len(state[chunk])) if done.get((chunk, i)) == place + 1]
            ) < len(state[chunk]):
                return
            for index in range(len(state[chunk])):
                done.pop((chunk, index), None)
            labels[chunk] = labels[chunk][:spot] + labels[chunk][spot + 1 :]
        done[(chunk, None)] = place + 1

    ran = 0
    for event in EVENTS:
        if event == "couple":
            if ran < parts:
                run_couple(ran)
                ran += 1
        elif ran == parts or (event[1] is not None and event[1] < ran):
            run(*event)
    while ran < parts:
        run_couple(ran)
        ran += 1
    for _ in range(2 * clus_bits + 2 * blk_bits + 2 * parts):
        for chunk in range(len(PLAN)):
            run(chunk)
    parts = []
    for ((keep, recv),) in state:
        parts += [v.reshape(clus_dev, -1, right) for v in (keep, recv)]
    turned = tangent.transpose(0, 3, 1, 2).reshape(clus_dev, tiles, 9)
    out = finish(turned, parts, cuts, piece)
    return out.transpose(0, 2, 1, 3)


def solution(mesh):
    placed = (
        P("clus", "blk", None, None),
        P("clus", "blk", None, None),
        P("clus"),
        P("clus", None),
        P("clus"),
        P("clus", None, None, "blk"),
    )
    return jax.shard_map(
        local, mesh=mesh, in_specs=placed, out_specs=P("clus", "blk", None, None), check_vma=False
    )
```

```python
import functools

import jax
import jax.numpy as jnp
from jax import lax
from jax.experimental import pallas as pl
from jax.experimental.pallas import tpu as pltpu
from jax.sharding import PartitionSpec as P


PLAN = ((10, 'b012'), (9, '1b02'), (8, 'b012'), (9, '012b'))

EVENTS = ('couple', (2, 0), (3, None), (1, None), (0, 0), (2, None), (3, None), (1, None), (0, None), (2, None), (3, None), (1, None), (2, None), (0, None), (1, None), (3, None), (0, None))

PER = 6
PARTS = 1


def bits_of(size):
    return size.bit_length() - 1


def cut_rows(rows):
    whole = sum(share for share, _ in PLAN)
    edges, total = [0], 0
    for share, _ in PLAN:
        total += share
        edges.append(rows // 8 * total // whole * 8)
    edges[-1] = rows
    return list(zip(edges[:-1], edges[1:]))


def route(order, blk_bits, clus_bits):
    steps = []
    for letter in order:
        if letter == "b":
            steps += [("blk", bit) for bit in range(1, blk_bits)]
        elif int(letter) < clus_bits:
            steps.append(("clus", int(letter)))
    named = [bit for axis, bit in steps if axis == "clus"]
    return steps + [("clus", bit) for bit in range(clus_bits) if bit not in named]


def couple_kernel(cuts, piece, halves, aliased, row_ref, side_ref, adjoint_ref, block_ref, *rest):
    outs, result_ref = rest[aliased:-1], rest[-1]
    per = block_ref.shape[0]
    first = pl.program_id(0) * per
    side = side_ref[0]
    for inner in range(per):
        lam = adjoint_ref[row_ref[first + inner]]
        result_ref[inner] = lax.dot_general(
            lam, block_ref[inner], (((0,), (0,)), ((), ())), preferred_element_type=jnp.float32
        ).T
        for index, (begin, end) in enumerate(cuts):
            for half in range(halves):
                away = pl.multiple_of((2 * half + 1 - side) * piece + begin, 8)
                home = pl.multiple_of((2 * half + side) * piece + begin, 8)
                outs[2 * index][half, inner] = result_ref[inner, pl.ds(away, end - begin), :]
                outs[2 * index + 1][half, inner] = result_ref[inner, pl.ds(home, end - begin), :]


def couple(adjoint, blocks, rows, side, cuts, early, piece, halves, part, held):
    pairs, depth, width = blocks.shape
    clus_dev, _, right = adjoint.shape
    count = rows.shape[0]
    per = next(n for n in (PER, 4, 3, 2, 1) if count % n == 0)
    jump = part * count // per
    shapes, specs, aliases, extra = [], [], {}, []
    for (begin, end), alone in zip(cuts, early):
        for _ in range(2):
            shape = (halves, count if alone else pairs, end - begin, right)
            if not alone and part > 0:
                aliases[4 + len(extra)] = len(shapes)
                extra.append(held[len(shapes)])
            shapes.append(pltpu.HBM(shape, jnp.float32))
            move = 0 if alone else jump
            specs.append(
                pl.BlockSpec(
                    (halves, per, end - begin, right),
                    lambda p, rows, side, move=move: (0, p + move, 0, 0),
                )
            )
    grant = 4 * per * width * (depth + 3 * right) + (3 << 20)
    return pl.pallas_call(
        functools.partial(couple_kernel, cuts, piece, halves, len(extra)),
        out_shape=shapes,
        grid_spec=pltpu.PrefetchScalarGridSpec(
            num_scalar_prefetch=2,
            grid=(count // per,),
            in_specs=[
                pl.BlockSpec((clus_dev, depth, right), lambda p, rows, side: (0, 0, 0)),
                pl.BlockSpec((per, depth, width), lambda p, rows, side: (p + jump, 0, 0)),
            ]
            + [pl.BlockSpec(memory_space=pl.ANY)] * len(extra),
            out_specs=specs,
            scratch_shapes=[pltpu.VMEM((per, width, right), jnp.float32)],
        ),
        input_output_aliases=aliases,
        name="couple",
        compiler_params=pltpu.CompilerParams(vmem_limit_bytes=grant),
        cost_estimate=pl.CostEstimate(
            flops=2 * count * depth * width * right,
            bytes_accessed=count * width * (2 * depth + 4 * right),
            transcendentals=0,
        ),
    )(
        pltpu.with_memory_space_constraint(rows, pltpu.HBM),
        side,
        pltpu.with_memory_space_constraint(adjoint, pltpu.HBM),
        pltpu.with_memory_space_constraint(blocks, pltpu.HBM),
        *extra,
    )


def gather_kernel(parts, slot_ref, *rest):
    values, (send_ref, home_ref, total_ref) = rest[: 2 * parts], rest[2 * parts :]
    total_ref[...] = jnp.zeros_like(total_ref)
    for part in range(parts):
        keep_ref, recv_ref = values[2 * part], values[2 * part + 1]
        count = keep_ref.shape[1]

        def add(pair, carry):
            slot = slot_ref[part * count + pair]
            total_ref[slot] += keep_ref[0, pair] + recv_ref[0, pair]
            return carry

        lax.fori_loop(0, count, add, 0, unroll=4)
    half = send_ref.shape[1]
    send_ref[0] = total_ref[:half]
    home_ref[0] = total_ref[half:]


def row_step(rows):
    best = 8
    for step in range(8, min(rows, 96) + 1, 8):
        if rows % step == 0:
            best = step
    return best


def gather_slots(slots, values, half):
    lead, count, rows, right = values[0].shape
    pairs = slots.shape[0]
    step = row_step(rows)
    shape = jax.ShapeDtypeStruct((lead, half, rows, right), jnp.float32)
    read = pl.BlockSpec((1, count, step, right), lambda a, r, s: (a, 0, r, 0))
    write = pl.BlockSpec((1, half, step, right), lambda a, r, s: (a, 0, r, 0))
    grant = 16 * step * right * (2 * pairs + 3 * half) + (2 << 20)
    return pl.pallas_call(
        functools.partial(gather_kernel, len(values) // 2),
        out_shape=[shape, shape],
        grid_spec=pltpu.PrefetchScalarGridSpec(
            num_scalar_prefetch=1,
            grid=(lead, rows // step),
            in_specs=[read] * len(values),
            out_specs=[write, write],
            scratch_shapes=[pltpu.VMEM((2 * half, step, right), jnp.float32)],
        ),
        name="gather_slots",
        compiler_params=pltpu.CompilerParams(vmem_limit_bytes=grant),
        cost_estimate=pl.CostEstimate(
            flops=2 * lead * pairs * rows * right,
            bytes_accessed=8 * lead * (pairs + half) * rows * right,
            transcendentals=0,
        ),
    )(slots, *values)


def finish_kernel(cuts, tangent_ref, *rest):
    parts, out_ref, field_ref = rest[:-2], rest[-2], rest[-1]
    for index, (begin, end) in enumerate(cuts):
        field_ref[begin:end] = parts[2 * index][0] + parts[2 * index + 1][0]
    tiles = out_ref.shape[2]
    field = [field_ref[pl.ds(comp, tiles, stride=3), :] for comp in range(3)]
    for out_comp in range(3):
        accum = tangent_ref[0, :, out_comp : out_comp + 1] * field[0]
        for in_comp in range(1, 3):
            place = 3 * in_comp + out_comp
            accum = accum + tangent_ref[0, :, place : place + 1] * field[in_comp]
        out_ref[0, out_comp] = accum


def finish(tangent, parts, cuts, piece):
    clus_dev, tiles, nine = tangent.shape
    right = parts[0].shape[-1]
    specs = [pl.BlockSpec((1, tiles, nine), lambda c: (c, 0, 0))]
    for part in parts:
        specs.append(pl.BlockSpec((1, part.shape[1], right), lambda c: (c, 0, 0)))
    return pl.pallas_call(
        functools.partial(finish_kernel, cuts),
        out_shape=jax.ShapeDtypeStruct((clus_dev, 3, tiles, right), jnp.float32),
        grid=(clus_dev,),
        in_specs=specs,
        out_specs=pl.BlockSpec((1, 3, tiles, right), lambda c: (c, 0, 0, 0)),
        scratch_shapes=[pltpu.VMEM((piece, right), jnp.float32)],
        name="finish",
        compiler_params=pltpu.CompilerParams(vmem_limit_bytes=8 << 20),
        cost_estimate=pl.CostEstimate(
            flops=18 * clus_dev * tiles * right,
            bytes_accessed=48 * clus_dev * tiles * right,
            transcendentals=0,
        ),
    )(tangent, *parts)


def local(adjoint, blocks, row_cluster, col_owner, col_cluster, tangent):
    pairs, tiles, comps, width = blocks.shape
    clus_dev, right = adjoint.shape[0], adjoint.shape[3]
    sizes = {"clus": lax.axis_size("clus"), "blk": lax.axis_size("blk")}
    here = {"clus": lax.axis_index("clus"), "blk": lax.axis_index("blk")}
    clus_bits, blk_bits = bits_of(sizes["clus"]), bits_of(sizes["blk"])
    piece = width // sizes["blk"]
    halves = sizes["blk"] // 2
    cuts = cut_rows(piece)
    owner = col_owner[:, 0]

    def my_bit(axis, bit):
        return (here[axis] >> bit) & 1

    def swap(value, axis, bit):
        return lax.ppermute(value, axis, [(i, i ^ (1 << bit)) for i in range(sizes[axis])])

    flat_adjoint = adjoint.transpose(0, 2, 1, 3).reshape(clus_dev, comps * tiles, right)
    flat_blocks = blocks.transpose(0, 2, 1, 3).reshape(pairs, comps * tiles, width)
    side = my_bit("blk", 0).astype(jnp.int32).reshape(1)
    half = sizes["clus"] * clus_dev // 2
    routes = [route(order, blk_bits, clus_bits) for _, order in PLAN]
    early = [steps[0][0] == "blk" for steps in routes]
    parts = next(n for n in (PARTS, 2, 1) if pairs % n == 0)
    count = pairs // parts

    def slots_for(bit):
        apart = (owner >> bit) & 1
        other = ((owner >> (bit + 1)) << bit) | (owner & ((1 << bit) - 1))
        home = (apart == my_bit("clus", bit)).astype(jnp.int32)
        return home * half + other * clus_dev + col_cluster

    def split(keep, recv, lead, axis, bit):
        rows = keep.shape[-2]
        both = [v.reshape(lead, 2, -1, rows, right) for v in (keep, recv)]
        mine = my_bit(axis, bit)

        def pick(which):
            left, other = (lax.dynamic_index_in_dim(v, which, 1, keepdims=False) for v in both)
            return left + other

        send, home = pick(1 - mine), pick(mine)
        recv = swap(send, axis, bit)
        return home, recv.reshape(home.shape)

    state = [None] * len(PLAN)
    used = [event[0] for event in EVENTS if event != "couple"]
    first_use = sorted(range(len(PLAN)), key=lambda c: used.index(c) if c in used else len(used))
    held = None

    def run_couple(part):
        nonlocal held
        rows = lax.slice_in_dim(row_cluster, part * count, (part + 1) * count)
        held = couple(flat_adjoint, flat_blocks, rows, side, cuts, early, piece, halves, part, held)
        for chunk in first_use:
            send, keep = held[2 * chunk], held[2 * chunk + 1]
            if early[chunk] or part == parts - 1:
                recv = swap(send, "blk", 0)
                state[chunk] = (state[chunk] or []) + [(keep, recv)]

    labels = [[("blk", bit) for bit in range(blk_bits - 1, 0, -1)] + ["pairs"] for _ in PLAN]
    done = {}

    def run(chunk, part=None):
        place = done.get((chunk, part), done.get((chunk, None), 0))
        if part is not None and (
            (chunk, part) in done or "pairs" not in labels[chunk] or part >= len(state[chunk])
        ):
            return
        if place >= len(routes[chunk]):
            return
        axis, bit = routes[chunk][place]
        if axis == "clus" and "pairs" in labels[chunk]:
            values = []
            for pair in state[chunk]:
                values += [v.reshape(-1, *v.shape[-3:]) for v in pair]
            slots = slots_for(bit)
            send, home = gather_slots(slots, values, half)
            recv = swap(send, axis, bit)
            labels[chunk] = labels[chunk][:-1] + [
                ("clus", b) for b in range(clus_bits - 1, -1, -1) if b != bit
            ] + ["own"]
            state[chunk] = [(home, recv)]
        else:
            spot = labels[chunk].index((axis, bit))
            which = range(len(state[chunk])) if part is None else [part]
            for index in which:
                if (chunk, index) in done and part is None and "pairs" in labels[chunk]:
                    continue
                state[chunk][index] = split(*state[chunk][index], 2**spot, axis, bit)
                if "pairs" in labels[chunk]:
                    done[(chunk, index)] = place + 1
            if "pairs" in labels[chunk] and len(
                [i for i in range(len(state[chunk])) if done.get((chunk, i)) == place + 1]
            ) < len(state[chunk]):
                return
            for index in range(len(state[chunk])):
                done.pop((chunk, index), None)
            labels[chunk] = labels[chunk][:spot] + labels[chunk][spot + 1 :]
        done[(chunk, None)] = place + 1

    ran = 0
    for event in EVENTS:
        if event == "couple":
            if ran < parts:
                run_couple(ran)
                ran += 1
        elif ran == parts or (event[1] is not None and event[1] < ran):
            run(*event)
    while ran < parts:
        run_couple(ran)
        ran += 1
    for _ in range(2 * clus_bits + 2 * blk_bits + 2 * parts):
        for chunk in range(len(PLAN)):
            run(chunk)
    parts = []
    for ((keep, recv),) in state:
        parts += [v.reshape(clus_dev, -1, right) for v in (keep, recv)]
    turned = tangent.transpose(0, 3, 1, 2).reshape(clus_dev, tiles, 9)
    out = finish(turned, parts, cuts, piece)
    return out.transpose(0, 2, 1, 3)


def solution(mesh):
    placed = (
        P("clus", "blk", None, None),
        P("clus", "blk", None, None),
        P("clus"),
        P("clus", None),
        P("clus"),
        P("clus", None, None, "blk"),
    )
    return jax.shard_map(
        local, mesh=mesh, in_specs=placed, out_specs=P("clus", "blk", None, None), check_vma=False
    )
```

```python
import functools

import jax
import jax.numpy as jnp
from jax import lax
from jax.experimental import pallas as pl
from jax.experimental.pallas import tpu as pltpu
from jax.sharding import PartitionSpec as P


PLAN = ((9, 'b012'), (8, '1b02'), (9, 'b012'), (10, '01b2'))

EVENTS = ('couple', (2, 0), (3, None), (1, None), (0, 0), (2, None), (3, None), (1, None), (0, None), (2, None), (3, None), (1, None), (2, None), (3, None), (0, None), (1, None), (0, None))

PER = 6
COLUMNS = 256
PARTS = 1


def bits_of(size):
    return size.bit_length() - 1


def cut_rows(rows):
    whole = sum(share for share, _ in PLAN)
    edges, total = [0], 0
    for share, _ in PLAN:
        total += share
        edges.append(rows // 8 * total // whole * 8)
    edges[-1] = rows
    return list(zip(edges[:-1], edges[1:]))


def route(order, blk_bits, clus_bits):
    steps = []
    for letter in order:
        if letter == "b":
            steps += [("blk", bit) for bit in range(1, blk_bits)]
        elif int(letter) < clus_bits:
            steps.append(("clus", int(letter)))
    named = [bit for axis, bit in steps if axis == "clus"]
    return steps + [("clus", bit) for bit in range(clus_bits) if bit not in named]


def couple_kernel(cuts, piece, halves, aliased, row_ref, side_ref, adjoint_ref, block_ref, *rest):
    outs = rest[aliased:]
    per, _, width = block_ref.shape
    first = pl.program_id(0) * per

    def emit(side):
        for inner in range(per):
            lam = adjoint_ref[row_ref[first + inner]].T
            for left in range(0, width, COLUMNS):
                right = min(left + COLUMNS, width)
                value = jnp.dot(
                    lam, block_ref[inner, :, left:right], preferred_element_type=jnp.float32
                ).T
                for owner in range(2 * halves):
                    place = 1 if owner % 2 == side else 0
                    for index, (begin, end) in enumerate(cuts):
                        low = max(left, owner * piece + begin)
                        high = min(right, owner * piece + end)
                        if low < high:
                            start = low - owner * piece - begin
                            outs[2 * index + place][
                                owner // 2, inner, start : start + high - low
                            ] = value[low - left : high - left]

    for side in range(2):
        pl.when(side_ref[0] == side)(functools.partial(emit, side))


def couple(adjoint, blocks, rows, side, cuts, early, piece, halves, part, held):
    pairs, depth, width = blocks.shape
    clus_dev, _, right = adjoint.shape
    count = rows.shape[0]
    per = next(n for n in (PER, 4, 3, 2, 1) if count % n == 0)
    jump = part * count // per
    shapes, specs, aliases, extra = [], [], {}, []
    for (begin, end), alone in zip(cuts, early):
        for _ in range(2):
            shape = (halves, count if alone else pairs, end - begin, right)
            if not alone and part > 0:
                aliases[4 + len(extra)] = len(shapes)
                extra.append(held[len(shapes)])
            shapes.append(pltpu.HBM(shape, jnp.float32))
            move = 0 if alone else jump
            specs.append(
                pl.BlockSpec(
                    (halves, per, end - begin, right),
                    lambda p, rows, side, move=move: (0, p + move, 0, 0),
                )
            )
    grant = 4 * per * width * (depth + 3 * right) + (3 << 20)
    return pl.pallas_call(
        functools.partial(couple_kernel, cuts, piece, halves, len(extra)),
        out_shape=shapes,
        grid_spec=pltpu.PrefetchScalarGridSpec(
            num_scalar_prefetch=2,
            grid=(count // per,),
            in_specs=[
                pl.BlockSpec((clus_dev, depth, right), lambda p, rows, side: (0, 0, 0)),
                pl.BlockSpec((per, depth, width), lambda p, rows, side: (p + jump, 0, 0)),
            ]
            + [pl.BlockSpec(memory_space=pl.ANY)] * len(extra),
            out_specs=specs,
        ),
        input_output_aliases=aliases,
        name="couple",
        compiler_params=pltpu.CompilerParams(vmem_limit_bytes=grant),
        cost_estimate=pl.CostEstimate(
            flops=2 * count * depth * width * right,
            bytes_accessed=count * width * (2 * depth + 4 * right),
            transcendentals=0,
        ),
    )(
        pltpu.with_memory_space_constraint(rows, pltpu.HBM),
        side,
        pltpu.with_memory_space_constraint(adjoint, pltpu.HBM),
        pltpu.with_memory_space_constraint(blocks, pltpu.HBM),
        *extra,
    )


def gather_kernel(parts, slot_ref, *rest):
    values, (send_ref, home_ref, total_ref) = rest[: 2 * parts], rest[2 * parts :]
    total_ref[...] = jnp.zeros_like(total_ref)
    for part in range(parts):
        keep_ref, recv_ref = values[2 * part], values[2 * part + 1]
        count = keep_ref.shape[1]

        def add(pair, carry):
            slot = slot_ref[part * count + pair]
            total_ref[slot] += keep_ref[0, pair] + recv_ref[0, pair]
            return carry

        lax.fori_loop(0, count, add, 0, unroll=4)
    half = send_ref.shape[1]
    send_ref[0] = total_ref[:half]
    home_ref[0] = total_ref[half:]


def row_step(rows):
    best = 8
    for step in range(8, min(rows, 96) + 1, 8):
        if rows % step == 0:
            best = step
    return best


def gather_slots(slots, values, half):
    lead, count, rows, right = values[0].shape
    pairs = slots.shape[0]
    step = row_step(rows)
    shape = jax.ShapeDtypeStruct((lead, half, rows, right), jnp.float32)
    read = pl.BlockSpec((1, count, step, right), lambda a, r, s: (a, 0, r, 0))
    write = pl.BlockSpec((1, half, step, right), lambda a, r, s: (a, 0, r, 0))
    grant = 16 * step * right * (2 * pairs + 3 * half) + (2 << 20)
    return pl.pallas_call(
        functools.partial(gather_kernel, len(values) // 2),
        out_shape=[shape, shape],
        grid_spec=pltpu.PrefetchScalarGridSpec(
            num_scalar_prefetch=1,
            grid=(lead, rows // step),
            in_specs=[read] * len(values),
            out_specs=[write, write],
            scratch_shapes=[pltpu.VMEM((2 * half, step, right), jnp.float32)],
        ),
        name="gather_slots",
        compiler_params=pltpu.CompilerParams(vmem_limit_bytes=grant),
        cost_estimate=pl.CostEstimate(
            flops=2 * lead * pairs * rows * right,
            bytes_accessed=8 * lead * (pairs + half) * rows * right,
            transcendentals=0,
        ),
    )(slots, *values)


def finish_kernel(cuts, tangent_ref, *rest):
    parts, out_ref, field_ref = rest[:-2], rest[-2], rest[-1]
    for index, (begin, end) in enumerate(cuts):
        field_ref[begin:end] = parts[2 * index][0] + parts[2 * index + 1][0]
    tiles = out_ref.shape[2]
    field = [field_ref[pl.ds(comp, tiles, stride=3), :] for comp in range(3)]
    for out_comp in range(3):
        accum = tangent_ref[0, :, out_comp : out_comp + 1] * field[0]
        for in_comp in range(1, 3):
            place = 3 * in_comp + out_comp
            accum = accum + tangent_ref[0, :, place : place + 1] * field[in_comp]
        out_ref[0, out_comp] = accum


def finish(tangent, parts, cuts, piece):
    clus_dev, tiles, nine = tangent.shape
    right = parts[0].shape[-1]
    specs = [pl.BlockSpec((1, tiles, nine), lambda c: (c, 0, 0))]
    for part in parts:
        specs.append(pl.BlockSpec((1, part.shape[1], right), lambda c: (c, 0, 0)))
    return pl.pallas_call(
        functools.partial(finish_kernel, cuts),
        out_shape=jax.ShapeDtypeStruct((clus_dev, 3, tiles, right), jnp.float32),
        grid=(clus_dev,),
        in_specs=specs,
        out_specs=pl.BlockSpec((1, 3, tiles, right), lambda c: (c, 0, 0, 0)),
        scratch_shapes=[pltpu.VMEM((piece, right), jnp.float32)],
        name="finish",
        compiler_params=pltpu.CompilerParams(vmem_limit_bytes=8 << 20),
        cost_estimate=pl.CostEstimate(
            flops=18 * clus_dev * tiles * right,
            bytes_accessed=48 * clus_dev * tiles * right,
            transcendentals=0,
        ),
    )(tangent, *parts)


def local(adjoint, blocks, row_cluster, col_owner, col_cluster, tangent):
    pairs, tiles, comps, width = blocks.shape
    clus_dev, right = adjoint.shape[0], adjoint.shape[3]
    sizes = {"clus": lax.axis_size("clus"), "blk": lax.axis_size("blk")}
    here = {"clus": lax.axis_index("clus"), "blk": lax.axis_index("blk")}
    clus_bits, blk_bits = bits_of(sizes["clus"]), bits_of(sizes["blk"])
    piece = width // sizes["blk"]
    halves = sizes["blk"] // 2
    cuts = cut_rows(piece)
    owner = col_owner[:, 0]

    def my_bit(axis, bit):
        return (here[axis] >> bit) & 1

    def swap(value, axis, bit):
        return lax.ppermute(value, axis, [(i, i ^ (1 << bit)) for i in range(sizes[axis])])

    flat_adjoint = adjoint.transpose(0, 2, 1, 3).reshape(clus_dev, comps * tiles, right)
    flat_blocks = blocks.transpose(0, 2, 1, 3).reshape(pairs, comps * tiles, width)
    side = my_bit("blk", 0).astype(jnp.int32).reshape(1)
    half = sizes["clus"] * clus_dev // 2
    routes = [route(order, blk_bits, clus_bits) for _, order in PLAN]
    early = [steps[0][0] == "blk" for steps in routes]
    parts = next(n for n in (PARTS, 2, 1) if pairs % n == 0)
    count = pairs // parts

    def slots_for(bit):
        apart = (owner >> bit) & 1
        other = ((owner >> (bit + 1)) << bit) | (owner & ((1 << bit) - 1))
        home = (apart == my_bit("clus", bit)).astype(jnp.int32)
        return home * half + other * clus_dev + col_cluster

    def split(keep, recv, lead, axis, bit, together):
        rows = keep.shape[-2]
        both = [v.reshape(lead, 2, -1, rows, right) for v in (keep, recv)]
        mine = my_bit(axis, bit)

        def pick(which):
            left, other = (lax.dynamic_index_in_dim(v, which, 1, keepdims=False) for v in both)
            return left + other

        send = pick(1 - mine)
        if together:
            home = pick(mine)
        recv = swap(send, axis, bit)
        if not together:
            *both, _ = lax.optimization_barrier((*both, send))
            home = pick(mine)
        return home, recv.reshape(home.shape)

    state = [None] * len(PLAN)
    used = [event[0] for event in EVENTS if event != "couple"]
    first_use = sorted(range(len(PLAN)), key=lambda c: used.index(c) if c in used else len(used))
    held = None

    def run_couple(part):
        nonlocal held
        rows = lax.slice_in_dim(row_cluster, part * count, (part + 1) * count)
        held = couple(flat_adjoint, flat_blocks, rows, side, cuts, early, piece, halves, part, held)
        for chunk in first_use:
            send, keep = held[2 * chunk], held[2 * chunk + 1]
            if early[chunk] or part == parts - 1:
                recv = swap(send, "blk", 0)
                state[chunk] = (state[chunk] or []) + [(keep, recv)]

    labels = [[("blk", bit) for bit in range(blk_bits - 1, 0, -1)] + ["pairs"] for _ in PLAN]
    done = {}

    def run(chunk, part=None):
        place = done.get((chunk, part), done.get((chunk, None), 0))
        if part is not None and (
            (chunk, part) in done or "pairs" not in labels[chunk] or part >= len(state[chunk])
        ):
            return
        if place >= len(routes[chunk]):
            return
        axis, bit = routes[chunk][place]
        if axis == "clus" and "pairs" in labels[chunk]:
            values = []
            for pair in state[chunk]:
                values += [v.reshape(-1, *v.shape[-3:]) for v in pair]
            slots = slots_for(bit)
            send, home = gather_slots(slots, values, half)
            recv = swap(send, axis, bit)
            labels[chunk] = labels[chunk][:-1] + [
                ("clus", b) for b in range(clus_bits - 1, -1, -1) if b != bit
            ] + ["own"]
            state[chunk] = [(home, recv)]
        else:
            spot = labels[chunk].index((axis, bit))
            which = range(len(state[chunk])) if part is None else [part]
            for index in which:
                if (chunk, index) in done and part is None and "pairs" in labels[chunk]:
                    continue
                state[chunk][index] = split(
                    *state[chunk][index], 2**spot, axis, bit, "pairs" in labels[chunk]
                )
                if "pairs" in labels[chunk]:
                    done[(chunk, index)] = place + 1
            if "pairs" in labels[chunk] and len(
                [i for i in range(len(state[chunk])) if done.get((chunk, i)) == place + 1]
            ) < len(state[chunk]):
                return
            for index in range(len(state[chunk])):
                done.pop((chunk, index), None)
            labels[chunk] = labels[chunk][:spot] + labels[chunk][spot + 1 :]
        done[(chunk, None)] = place + 1

    ran = 0
    for event in EVENTS:
        if event == "couple":
            if ran < parts:
                run_couple(ran)
                ran += 1
        elif ran == parts or (event[1] is not None and event[1] < ran):
            run(*event)
    while ran < parts:
        run_couple(ran)
        ran += 1
    for _ in range(2 * clus_bits + 2 * blk_bits + 2 * parts):
        for chunk in range(len(PLAN)):
            run(chunk)
    parts = []
    for ((keep, recv),) in state:
        parts += [v.reshape(clus_dev, -1, right) for v in (keep, recv)]
    turned = tangent.transpose(0, 3, 1, 2).reshape(clus_dev, tiles, 9)
    out = finish(turned, parts, cuts, piece)
    return out.transpose(0, 2, 1, 3)


def solution(mesh):
    placed = (
        P("clus", "blk", None, None),
        P("clus", "blk", None, None),
        P("clus"),
        P("clus", None),
        P("clus"),
        P("clus", None, None, "blk"),
    )
    return jax.shard_map(
        local, mesh=mesh, in_specs=placed, out_specs=P("clus", "blk", None, None), check_vma=False
    )
```
